32 devices in a mesh: depth: 8 (over y, x, core), tile: 4 (over z).
Axes of the slice: x: 2, y: 2, z: 4, core: 2. Of those that a mesh axis runs over, the one named last changes fastest.
Arguments:
- measured: float32 [32, 1024, 1024], P('depth', 'tile'), may hold values from 0.1 to 3
- estimate: float32 [32, 1024, 1024], P('depth', 'tile'), may hold values from 0.5 to 2
- extinction: float32 [32, 1024, 1024], P('depth', 'tile'), may hold values from 0.002 to 0.05
- psf_rows: float32 [16, 65], replicated, may hold values from 0.05 to 1
- psf_cols: float32 [16, 65], replicated, may hold values from 0.05 to 1
- stratum: int32 [32], P('depth'), may hold values from 0 to 15
- seam_flags: int32 [3], replicated, may hold values 0 or 1
Outputs:
- updated: float32 [32, 1024, 1024], P('depth', 'tile')
- projection: float32 [1024, 1024], P('tile')
The draws below stay inside these ranges and needn't reach their ends.
All inputs are finite; a program needn't handle non-finite values.
Results may differ from the reference program's by a relative error of at most 0.000073.
Values sent between devices are 32-bit elements; how exact they have to be, the bound alone decides.
A program may use at most 128 MiB of HBM per device.

```python
import math
import jax
import jax.numpy as jnp
from jax import lax

ROWS_DEV = 256
NX = 1024
HALF = 32
TAPS = 65
STRATA = 16
NZ = 32
NY = 1024
N_TILE = 4


def touch_ends(array, key, smallest, high):
    spot = [jax.random.randint(jax.random.fold_in(key, axis), (), 0, length) for axis, length in enumerate(array.shape)]
    widest = array.shape.index(max(array.shape))
    beside = spot[:widest] + [(spot[widest] + 1) % array.shape[widest]] + spot[widest + 1:]
    return array.at[tuple(spot)].set(smallest).at[tuple(beside)].set(high)


def block_levels(stream_key, extent, shards, low, high):
    def one(axis_at, shards_of):
        heights = jax.random.uniform(jax.random.fold_in(jax.random.fold_in(stream_key, 6), axis_at), (shards_of,), jnp.float32, low / len(shards), high / len(shards))
        return jnp.repeat(jnp.exp(heights), extent[axis_at] // shards_of).reshape((-1,) + (1,) * (len(extent) - axis_at - 1))

    gain = one(*shards[0])
    for cut in shards[1:]:
        gain = gain * one(*cut)
    return gain


def setup_inputs(seed: int = 0) -> dict:
    keys = jax.random.split(jax.random.key(seed), 8)
    measured = jnp.clip(jnp.exp(math.log(3.0) - 3.4011974 * jax.random.uniform(keys[0], (NZ, NY, NX), jnp.float32) ** block_levels(keys[0], (NZ, NY, NX), ((0, 8), (1, 4)), -0.2, 0.2)), 0.1, 3.0)
    estimate = jnp.clip(0.5 + 1.5 * jax.random.uniform(keys[1], (NZ, NY, NX), jnp.float32) ** block_levels(keys[1], (NZ, NY, NX), ((0, 8), (1, 4)), -0.2, 0.2), 0.5, 2.0)
    extinction = jnp.clip(jnp.exp(math.log(0.05) - 3.218876 * jax.random.uniform(keys[2], (NZ, NY, NX), jnp.float32) ** block_levels(keys[2], (NZ, NY, NX), ((0, 8), (1, 4)), -0.2, 0.2)), 0.002, 0.05)
    psf_rows = jnp.clip(jnp.exp(jax.random.uniform(keys[3], (STRATA, TAPS), jnp.float32, math.log(0.05), math.log(1.0))), 0.05, 1.0)
    psf_cols = jnp.clip(jnp.exp(jax.random.uniform(keys[4], (STRATA, TAPS), jnp.float32, math.log(0.05), math.log(1.0))), 0.05, 1.0)
    stratum = touch_ends(jax.random.randint(keys[5], (NZ,), 0, STRATA), jax.random.fold_in(keys[5], 1), 0, STRATA - 1).astype(jnp.int32)
    seam_flags = touch_ends((jax.random.randint(keys[6], (N_TILE - 1,), 0, 4) < 3).astype(jnp.int32), jax.random.fold_in(keys[6], 1), 0, 1)
    return {"measured": measured, "estimate": estimate, "extinction": extinction, "psf_rows": psf_rows, "psf_cols": psf_cols, "stratum": stratum, "seam_flags": seam_flags}


def banded(kernel, row_count, col_count, offset):
    length = kernel.shape[0]
    offsets = jnp.arange(col_count, dtype=jnp.int32)[None, :] - jnp.arange(row_count, dtype=jnp.int32)[:, None] + offset
    inside = (offsets >= 0) & (offsets < length)
    picked = kernel[jnp.clip(offsets, 0, length - 1).astype(jnp.int32)]
    return jnp.where(inside, picked, jnp.zeros_like(picked))


def reference(measured, estimate, extinction, psf_rows, psf_cols, stratum, seam_flags):
    optical = jnp.cumsum(extinction, axis=0) - extinction
    weighted = jnp.exp(-optical) * estimate
    vertical = psf_rows / jnp.sum(psf_rows, axis=1, keepdims=True)
    lateral = psf_cols / jnp.sum(psf_cols, axis=1, keepdims=True)
    segment = jnp.concatenate([jnp.zeros((1,), jnp.int32), jnp.cumsum(1 - seam_flags).astype(jnp.int32)])
    row_segment = segment[(jnp.arange(NY, dtype=jnp.int32) // ROWS_DEV).astype(jnp.int32)]
    joined = row_segment[:, None] == row_segment[None, :]
    highest = lax.Precision.HIGHEST

    def one_plane(inputs):
        plane_weighted, plane_measured, plane_estimate, index = inputs
        band_rows = banded(vertical[index], NY, NY, HALF)
        band_rows = jnp.where(joined, band_rows, jnp.zeros_like(band_rows))
        band_cols = banded(lateral[index], NX, NX, HALF)
        blurred = jnp.dot(jnp.dot(band_rows, plane_weighted, precision=highest), band_cols.T, precision=highest)
        quotient = plane_measured / blurred
        spread = jnp.dot(jnp.dot(band_rows.T, quotient, precision=highest), band_cols, precision=highest)
        return plane_estimate * spread

    updated = lax.map(one_plane, (weighted, measured, estimate, stratum))
    return updated, jnp.max(updated, axis=0)
```

```python
import functools

import jax
import jax.numpy as jnp
from jax import lax
from jax.experimental import pallas as pl
from jax.experimental.pallas import tpu as pltpu
from jax.sharding import PartitionSpec as P

MESH = pl.DeviceIdType.MESH
BLOCK = 256
SIDE = 128


def split(value):
    high = value.astype(jnp.bfloat16)
    low = (value - high.astype(jnp.float32)).astype(jnp.bfloat16)
    return high, low


def kernel(
    dims, base_rows, base_cols, seams, meas_hbm, est_hbm, ext_hbm, upd_hbm, proj_hbm,
    meas, est, ext, local, stacked, quot, upd, vband, lhigh, llow, mhigh, mlow,
    slab, pooled, carried, sums, message, landed, above, peak, mpool, mland,
    lhalo, fhalo, qhalo,
    in_sem, out_sem, hal_send, hal_recv, q_send, q_recv, col_send, col_recv,
):
    depth_count, tile_count, planes, rows, cols, reach = dims
    half = rows // 2
    bits = depth_count.bit_length() - 1
    rest = list(range(1, bits))
    orders = [rest, rest[::-1]] if len(rest) == 2 else [rest]
    part = half // len(orders)
    steps = len(rest)
    wide = rows + 2 * reach
    chunk = 32
    d = lax.axis_index("depth")
    t = lax.axis_index("tile")
    has_up = t > 0
    has_down = t < tile_count - 1
    up = jnp.maximum(t - 1, 0)
    down = jnp.minimum(t + 1, tile_count - 1)

    def bit(b):
        return (d // (1 << b)) % 2

    def partner(b):
        return d + (1 - 2 * bit(b)) * (1 << b)

    def loads(which, src, dst):
        return pltpu.make_async_copy(src, dst, in_sem.at[which])

    get_ext = loads(0, ext_hbm, ext)
    get_est = loads(1, est_hbm, est)
    get_meas = loads(2, meas_hbm, meas)
    get_ext.start()
    get_est.start()
    get_meas.start()

    barrier = pltpu.get_barrier_semaphore()
    for b in range(bits):
        pl.semaphore_signal(barrier, inc=1, device_id={"depth": partner(b)}, device_id_type=MESH)

    @pl.when(has_up)
    def _():
        pl.semaphore_signal(barrier, inc=1, device_id={"tile": up}, device_id_type=MESH)

    @pl.when(has_down)
    def _():
        pl.semaphore_signal(barrier, inc=1, device_id={"tile": down}, device_id_type=MESH)

    def remote(src, dst, send, recv, where):
        return pltpu.make_async_remote_copy(
            src_ref=src, dst_ref=dst, send_sem=send, recv_sem=recv, device_id=where, device_id_type=MESH
        )

    def halo_pair(head, tail, to_up, to_down, send, recv):
        return (
            remote(head, to_up, send(0), recv(1), {"tile": up}),
            remote(tail, to_down, send(1), recv(0), {"tile": down}),
        )

    def halo_start(pair):
        pl.when(has_up)(lambda: pair[0].start())
        pl.when(has_down)(lambda: pair[1].start())

    def halo_recv(pair):
        pl.when(has_up)(lambda: pair[1].wait_recv())
        pl.when(has_down)(lambda: pair[0].wait_recv())

    def halo_sent(pair):
        pl.when(has_up)(lambda: pair[0].wait_send())
        pl.when(has_down)(lambda: pair[1].wait_send())

    @pl.when(t == 0)
    def _():
        lhalo[0] = jnp.zeros(lhalo.shape[1:], jnp.float32)
        fhalo[0] = jnp.zeros(fhalo.shape[1:], jnp.float32)
        qhalo[0] = jnp.zeros(qhalo.shape[1:], jnp.float32)

    @pl.when(t == tile_count - 1)
    def _():
        lhalo[1] = jnp.zeros(lhalo.shape[1:], jnp.float32)
        fhalo[1] = jnp.zeros(fhalo.shape[1:], jnp.float32)
        qhalo[1] = jnp.zeros(qhalo.shape[1:], jnp.float32)

    def over(count, body, size=chunk):
        def one(i, _):
            body(pl.ds(pl.multiple_of(i * size, size), size))
            return 0

        lax.fori_loop(0, count // size, one, 0)

    get_ext.wait()

    def slab_sum(at):
        total = ext[0, at, :]
        for p in range(1, planes):
            total = total + ext[p, at, :]
        slab[at, :] = total

    over(rows, slab_sum)
    pl.semaphore_wait(barrier, bits + has_up.astype(jnp.int32) + has_down.astype(jnp.int32))

    core = bit(0)
    own = pl.multiple_of(core * half, half)
    other = pl.multiple_of((1 - core) * half, half)

    rs = remote(slab.at[pl.ds(other, half)], pooled, col_send.at[0], col_recv.at[0], {"depth": partner(0)})
    rs.start()
    get_est.wait()

    def local_weights(at):
        run = jnp.zeros((chunk, cols), jnp.float32)
        for p in range(planes):
            local[p, at, :] = jnp.exp(-run) * est[p, at, :]
            if p < planes - 1:
                run = run + ext[p, at, :]

    over(rows, local_weights)
    lpair = halo_pair(
        local.at[:, pl.ds(0, reach)], local.at[:, pl.ds(rows - reach, reach)], lhalo.at[1], lhalo.at[0],
        lambda i: hal_send.at[i], lambda i: hal_recv.at[i],
    )
    halo_start(lpair)
    rs.wait_recv()

    def pool(at):
        sums[at, :] = slab[pl.ds(own + at.start, chunk), :] + pooled[at, :]

    over(half, pool)

    hops = []
    for s in range(steps):
        row = []
        for g, order in enumerate(orders):
            where = pl.ds(g * part, part)
            at = 2 + s * len(orders) + g
            row.append(remote(
                message.at[s - 1, where] if s else sums.at[where], landed.at[s, where],
                col_send.at[at], col_recv.at[at], {"depth": partner(order[s])},
            ))
        hops.append(row)
    for hop in hops[0]:
        hop.start()

    up_flag = jnp.where(has_up, seams[up], 0).astype(jnp.float32)
    down_flag = jnp.where(has_down, seams[jnp.minimum(t, tile_count - 2)], 0).astype(jnp.float32)
    lane = lax.broadcasted_iota(jnp.int32, (rows, 4 * BLOCK), 1)
    third = jnp.where(lane < wide, lane, jnp.where(lane < 2 * wide, lane - wide, lane - 2 * wide))
    scale = jnp.where(third < reach, up_flag, jnp.where(third >= wide - reach, down_flag, 1.0))

    def bands(i, _):
        tall = jnp.broadcast_to(base_rows[i], (rows, 4 * BLOCK))
        tall = pltpu.roll(tall, 0, 1, stride=1, stride_axis=0) * scale
        high, low = split(tall)
        vband[i] = jnp.where(lane < 2 * wide, high.astype(jnp.float32), low.astype(jnp.float32)).astype(jnp.bfloat16)
        square = jnp.broadcast_to(base_cols[i], (2 * BLOCK, 2 * BLOCK))
        square = pltpu.roll(square, 0, 1, stride=1, stride_axis=0)[:, :BLOCK]
        high, low = split(square)
        lhigh[i] = high
        llow[i] = low
        return 0

    lax.fori_loop(0, 2 * planes, bands, 0)
    for m in (mhigh, mlow):
        m[:, :SIDE] = jnp.zeros((rows, SIDE), jnp.bfloat16)
        m[:, SIDE + cols:] = jnp.zeros((rows, SIDE), jnp.bfloat16)

    for s in range(steps):
        for g, order in enumerate(orders):
            hops[s][g].wait_recv()
            upper = bit(order[s]).astype(jnp.float32)
            ascending = s == 0 or order[s] > order[s - 1]

            def absorb(at, s=s, g=g, order=order, upper=upper, ascending=ascending):
                at = pl.ds(g * part + at.start, chunk)
                got = landed[s, at, :]
                if s == 0:
                    before = upper * got
                elif ascending:
                    before = carried[at, :] + upper * got
                else:
                    before = carried[at, :] + got
                carried[at, :] = before
                if s + 1 < steps:
                    if order[s + 1] > order[s]:
                        total = (sums[at, :] if s == 0 else message[s - 1, at, :]) + got
                        message[s, at, :] = total
                    else:
                        lower = 1.0 - bit(order[s + 1]).astype(jnp.float32)
                        message[s, at, :] = before + lower * sums[at, :]

            over(part, absorb)
            if s + 1 < steps:
                hops[s + 1][g].start()

    ag = remote(slab.at[pl.ds(own, half)], above.at[pl.ds(own, half)], col_send.at[1], col_recv.at[1], {"depth": partner(0)})
    first = core.astype(jnp.float32)

    def give(at):
        rest_at = pl.ds(own + at.start, chunk)
        before = carried[at, :]
        above[rest_at, :] = before + first * pooled[at, :]
        slab[rest_at, :] = before + (1.0 - first) * slab[rest_at, :]

    over(half, give)
    ag.start()
    ag.wait_recv()

    def fade(at):
        above[at, :] = jnp.exp(-above[at, :])

    over(rows, fade)
    fpair = halo_pair(
        above.at[pl.ds(0, reach)], above.at[pl.ds(rows - reach, reach)], fhalo.at[1], fhalo.at[0],
        lambda i: hal_send.at[2 + i], lambda i: hal_recv.at[2 + i],
    )
    halo_start(fpair)
    get_meas.wait()
    halo_recv(lpair)
    halo_recv(fpair)

    def put(value, start, size):
        high, low = split(value)
        stacked[pl.ds(start, size), :] = high
        stacked[pl.ds(wide + start, size), :] = low
        stacked[pl.ds(2 * wide + start, size), :] = high

    def blur(i, use):
        for n in range(cols // BLOCK):
            mixed = jnp.dot(
                vband[i, :, : 3 * wide], stacked[:, n * BLOCK : (n + 1) * BLOCK], preferred_element_type=jnp.float32
            )
            high, low = split(mixed)
            mhigh[:, SIDE + n * BLOCK : SIDE + (n + 1) * BLOCK] = high
            mlow[:, SIDE + n * BLOCK : SIDE + (n + 1) * BLOCK] = low
        for n in range(cols // BLOCK):
            def window(m):
                start = n * BLOCK
                return jnp.concatenate(
                    [m[:, start + SIDE : start + SIDE + BLOCK + SIDE], m[:, start : start + SIDE]], axis=1
                )

            high, low = window(mhigh), window(mlow)
            use(
                slice(n * BLOCK, (n + 1) * BLOCK),
                jnp.dot(high, lhigh[i], preferred_element_type=jnp.float32)
                + jnp.dot(low, lhigh[i], preferred_element_type=jnp.float32)
                + jnp.dot(high, llow[i], preferred_element_type=jnp.float32),
            )

    def qpair_of(p):
        return halo_pair(
            quot.at[p, pl.ds(0, reach)], quot.at[p, pl.ds(rows - reach, reach)], qhalo.at[1, p], qhalo.at[0, p],
            lambda i: q_send.at[i, p], lambda i: q_recv.at[i, p],
        )

    def forward(p, _):
        put(fhalo[0] * lhalo[0, p], 0, reach)
        put(fhalo[1] * lhalo[1, p], rows + reach, reach)

        def inner(at):
            put(above[at, :] * local[p, at, :], pl.multiple_of(at.start + reach, chunk), chunk)

        over(rows, inner)

        def use(at, blurred):
            quot[p, :, at] = meas[p, :, at] / blurred

        blur(p, use)
        halo_start(qpair_of(p))
        return 0

    lax.fori_loop(0, planes, forward, 0)

    def backward(p, _):
        halo_recv(qpair_of(p))
        put(qhalo[0, p], 0, reach)
        put(qhalo[1, p], rows + reach, reach)

        def inner(at):
            put(quot[p, at, :], pl.multiple_of(at.start + reach, chunk), chunk)

        over(rows, inner)

        def use(at, spread):
            upd[p, :, at] = est[p, :, at] * spread

        blur(planes + p, use)
        pltpu.make_async_copy(upd.at[p], upd_hbm.at[p], out_sem.at[p]).start()
        return 0

    lax.fori_loop(0, planes, backward, 0)

    def top(at):
        best = upd[0, at, :]
        for p in range(1, planes):
            best = jnp.maximum(best, upd[p, at, :])
        peak[at, :] = best

    over(rows, top)
    base = 2 + steps * len(orders)
    rs2 = remote(peak.at[pl.ds(other, half)], mpool.at[0], col_send.at[base], col_recv.at[base], {"depth": partner(0)})
    rs2.start()
    rs2.wait_recv()

    def merge(at):
        mpool[1, at, :] = jnp.maximum(mpool[0, at, :], peak[pl.ds(own + at.start, chunk), :])

    over(half, merge)
    hops2 = []
    for s in range(steps):
        row = []
        for g, order in enumerate(orders):
            where = pl.ds(g * part, part)
            at = base + 2 + s * len(orders) + g
            row.append(remote(
                mpool.at[1 + s, where], mland.at[s, where], col_send.at[at], col_recv.at[at],
                {"depth": partner(order[s])},
            ))
        hops2.append(row)
    for hop in hops2[0]:
        hop.start()
    for s in range(steps):
        for g in range(len(orders)):
            hops2[s][g].wait_recv()

            def keep(at, s=s, g=g):
                at = pl.ds(g * part + at.start, chunk)
                mpool[2 + s, at, :] = jnp.maximum(mpool[1 + s, at, :], mland[s, at, :])

            over(part, keep)
            if s + 1 < steps:
                hops2[s + 1][g].start()
    ag2 = remote(mpool.at[1 + steps], mland.at[steps], col_send.at[base + 1], col_recv.at[base + 1], {"depth": partner(0)})
    ag2.start()
    put_own = pltpu.make_async_copy(mpool.at[1 + steps], proj_hbm.at[pl.ds(own, half)], out_sem.at[planes])
    put_own.start()
    ag2.wait_recv()
    put_other = pltpu.make_async_copy(mland.at[steps], proj_hbm.at[pl.ds(other, half)], out_sem.at[planes + 1])
    put_other.start()

    rs.wait_send()
    ag.wait_send()
    rs2.wait_send()
    ag2.wait_send()
    for row in hops + hops2:
        for hop in row:
            hop.wait_send()
    halo_sent(lpair)
    halo_sent(fpair)
    for p in range(planes):
        halo_sent(qpair_of(p))
        pltpu.make_async_copy(upd.at[p], upd_hbm.at[p], out_sem.at[p]).wait()
    put_own.wait()
    put_other.wait()


def on_device(dims, measured, estimate, extinction, psf_rows, psf_cols, stratum, seam_flags):
    depth_count, tile_count, planes, rows, cols, reach = dims
    strata, length = psf_rows.shape
    wide = rows + 2 * reach
    picker = (stratum[:, None] == jnp.arange(strata, dtype=jnp.int32)[None, :])[:, :, None]

    def choose(psf):
        taps = psf / jnp.sum(psf, axis=1, keepdims=True)
        return jnp.sum(jnp.where(picker, taps[None], 0.0), axis=1)

    vertical, lateral = choose(psf_rows), choose(psf_cols)
    vertical = jnp.concatenate([vertical, vertical[:, ::-1]], axis=0)
    lateral = jnp.concatenate([lateral[:, ::-1], lateral], axis=0)
    third = jnp.pad(vertical, ((0, 0), (0, wide - length)))
    base_rows = jnp.pad(jnp.concatenate([third] * 3, axis=1), ((0, 0), (0, 4 * BLOCK - 3 * wide)))[:, None, :]
    gap = jnp.zeros((2 * planes, 2 * BLOCK - length), jnp.float32)
    base_cols = jnp.concatenate([lateral[:, reach:], gap, lateral[:, :reach]], axis=1)[:, None, :]

    half = rows // 2
    bits = depth_count.bit_length() - 1
    steps = bits - 1
    groups = 2 if steps == 2 else 1
    collectives = 2 * (2 + steps * groups)
    f32, bf16 = jnp.float32, jnp.bfloat16
    whole = (planes, rows, cols)
    return pl.pallas_call(
        functools.partial(kernel, dims),
        out_shape=(jax.ShapeDtypeStruct(whole, f32), jax.ShapeDtypeStruct((rows, cols), f32)),
        in_specs=[
            pl.BlockSpec(memory_space=pltpu.VMEM),
            pl.BlockSpec(memory_space=pltpu.VMEM),
            pl.BlockSpec(memory_space=pltpu.SMEM),
            pl.BlockSpec(memory_space=pl.ANY),
            pl.BlockSpec(memory_space=pl.ANY),
            pl.BlockSpec(memory_space=pl.ANY),
        ],
        out_specs=(pl.BlockSpec(memory_space=pl.ANY), pl.BlockSpec(memory_space=pl.ANY)),
        scratch_shapes=[
            pltpu.VMEM(whole, f32),
            pltpu.VMEM(whole, f32),
            pltpu.VMEM(whole, f32),
            pltpu.VMEM(whole, f32),
            pltpu.VMEM((3 * wide, cols), bf16),
            pltpu.VMEM(whole, f32),
            pltpu.VMEM(whole, f32),
            pltpu.VMEM((2 * planes, rows, 4 * BLOCK), bf16),
            pltpu.VMEM((2 * planes, 2 * BLOCK, BLOCK), bf16),
            pltpu.VMEM((2 * planes, 2 * BLOCK, BLOCK), bf16),
            pltpu.VMEM((rows, cols + 2 * SIDE), bf16),
            pltpu.VMEM((rows, cols + 2 * SIDE), bf16),
            pltpu.VMEM((rows, cols), f32),
            pltpu.VMEM((half, cols), f32),
            pltpu.VMEM((half, cols), f32),
            pltpu.VMEM((half, cols), f32),
            pltpu.VMEM((max(steps - 1, 1), half, cols), f32),
            pltpu.VMEM((steps, half, cols), f32),
            pltpu.VMEM((rows, cols), f32),
            pltpu.VMEM((rows, cols), f32),
            pltpu.VMEM((2 + steps, half, cols), f32),
            pltpu.VMEM((1 + steps, half, cols), f32),
            pltpu.VMEM((2, planes, reach, cols), f32),
            pltpu.VMEM((2, reach, cols), f32),
            pltpu.VMEM((2, planes, reach, cols), f32),
            pltpu.SemaphoreType.DMA((3,)),
            pltpu.SemaphoreType.DMA((planes + 2,)),
            pltpu.SemaphoreType.DMA((4,)),
            pltpu.SemaphoreType.DMA((4,)),
            pltpu.SemaphoreType.DMA((2, planes)),
            pltpu.SemaphoreType.DMA((2, planes)),
            pltpu.SemaphoreType.DMA((collectives,)),
            pltpu.SemaphoreType.DMA((collectives,)),
        ],
        compiler_params=pltpu.CompilerParams(
            collective_id=0, has_side_effects=True, vmem_limit_bytes=62 * 1024 * 1024
        ),
    )(base_rows, base_cols, seam_flags, measured, estimate, extinction)


def solution(mesh):
    def body(measured, estimate, extinction, psf_rows, psf_cols, stratum, seam_flags):
        planes, rows, cols = measured.shape
        dims = (mesh.shape["depth"], mesh.shape["tile"], planes, rows, cols, (psf_rows.shape[1] - 1) // 2)
        return on_device(dims, measured, estimate, extinction, psf_rows, psf_cols, stratum, seam_flags)

    return jax.shard_map(
        body,
        mesh=mesh,
        in_specs=(
            P("depth", "tile", None),
            P("depth", "tile", None),
            P("depth", "tile", None),
            P(),
            P(),
            P("depth"),
            P(),
        ),
        out_specs=(P("depth", "tile", None), P("tile", None)),
        check_vma=False,
    )
```

```python
import functools

import jax
import jax.numpy as jnp
from jax import lax
from jax.experimental import pallas as pl
from jax.experimental.pallas import tpu as pltpu
from jax.sharding import PartitionSpec as P

MESH = pl.DeviceIdType.MESH
BLOCK = 256
SIDE = 128


def split(value):
    high = value.astype(jnp.bfloat16)
    low = (value - high.astype(jnp.float32)).astype(jnp.bfloat16)
    return high, low


def kernel(
    dims, psf_rows, psf_cols, stratum, seams, meas_hbm, est_hbm, ext_hbm, upd, proj,
    meas, est, ext, local, stacked, tall_table, flat_table, vband, lhigh, llow, mhigh, mlow,
    slab, pooled, carried, sums, message, landed, above, peak, mpool, mland,
    lhalo, fhalo, qhalo,
    in_sem, hal_send, hal_recv, q_send, q_recv, col_send, col_recv,
):
    depth_count, tile_count, planes, rows, cols, reach = dims
    half = rows // 2
    bits = depth_count.bit_length() - 1
    rest = list(range(1, bits))
    orders = [rest, rest[::-1]] if len(rest) == 2 else [rest]
    part = half // len(orders)
    steps = len(rest)
    wide = rows + 2 * reach
    chunk = 64
    blocks = cols // BLOCK
    groups = len(orders)
    d = lax.axis_index("depth")
    t = lax.axis_index("tile")
    has_up = t > 0
    has_down = t < tile_count - 1
    up = jnp.maximum(t - 1, 0)
    down = jnp.minimum(t + 1, tile_count - 1)

    def bit(b):
        return (d // (1 << b)) % 2

    def partner(b):
        return d + (1 - 2 * bit(b)) * (1 << b)

    def loads(which, src, dst):
        return pltpu.make_async_copy(src, dst, in_sem.at[which])

    def span(n):
        return pl.ds(n * BLOCK, BLOCK)

    get_ext = [loads(2 + n, ext_hbm.at[:, :, span(n)], ext.at[:, :, span(n)]) for n in range(blocks)]
    get_est = loads(0, est_hbm, est)
    get_meas = loads(1, meas_hbm, meas)
    for n in range(blocks):
        get_ext[n].start()
    get_est.start()
    get_meas.start()

    barrier = pltpu.get_barrier_semaphore()
    for b in range(bits):
        pl.semaphore_signal(barrier, inc=1, device_id={"depth": partner(b)}, device_id_type=MESH)

    @pl.when(has_up)
    def _():
        pl.semaphore_signal(barrier, inc=1, device_id={"tile": up}, device_id_type=MESH)

    @pl.when(has_down)
    def _():
        pl.semaphore_signal(barrier, inc=1, device_id={"tile": down}, device_id_type=MESH)

    def remote(src, dst, send, recv, where):
        return pltpu.make_async_remote_copy(
            src_ref=src, dst_ref=dst, send_sem=send, recv_sem=recv, device_id=where, device_id_type=MESH
        )

    def halo_pair(head, tail, to_up, to_down, send, recv):
        return (
            remote(head, to_up, send(0), recv(1), {"tile": up}),
            remote(tail, to_down, send(1), recv(0), {"tile": down}),
        )

    def halo_start(pair):
        pl.when(has_up)(lambda: pair[0].start())
        pl.when(has_down)(lambda: pair[1].start())

    def halo_recv(pair):
        pl.when(has_up)(lambda: pair[1].wait_recv())
        pl.when(has_down)(lambda: pair[0].wait_recv())

    def halo_sent(pair):
        pl.when(has_up)(lambda: pair[0].wait_send())
        pl.when(has_down)(lambda: pair[1].wait_send())

    @pl.when(t == 0)
    def _():
        lhalo[0] = jnp.zeros(lhalo.shape[1:], jnp.float32)
        fhalo[0] = jnp.zeros(fhalo.shape[1:], jnp.float32)
        qhalo[0] = jnp.zeros(qhalo.shape[1:], jnp.float32)

    @pl.when(t == tile_count - 1)
    def _():
        lhalo[1] = jnp.zeros(lhalo.shape[1:], jnp.float32)
        fhalo[1] = jnp.zeros(fhalo.shape[1:], jnp.float32)
        qhalo[1] = jnp.zeros(qhalo.shape[1:], jnp.float32)

    def over(count, body, size=chunk):
        def one(i, _):
            body(pl.ds(pl.multiple_of(i * size, size), size))
            return 0

        lax.fori_loop(0, count // size, one, 0)

    core = bit(0)
    own = pl.multiple_of(core * half, half)
    other = pl.multiple_of((1 - core) * half, half)
    first = core.astype(jnp.float32)

    class Exchange:
        def __init__(self, base, source, mine, pooled, lead, relay, landed, finish, target):
            self.base = base
            self.rs = [self.copy(0, n, source.at[pl.ds(other, half), span(n)], pooled.at[:, span(n)], 0) for n in range(blocks)]
            self.hops = []
            for s in range(steps):
                level = []
                for n in range(blocks):
                    row = []
                    for g, order in enumerate(orders):
                        where = pl.ds(g * part, part)
                        src = relay.at[s - 1, where, span(n)] if s else lead.at[where, span(n)]
                        row.append(self.copy(2 + s * groups + g, n, src, landed.at[s, where, span(n)], order[s]))
                    level.append(row)
                self.hops.append(level)
            self.ag = [self.copy(1, n, finish(n), target.at[pl.ds(own, half), span(n)], 0) for n in range(blocks)]

        def copy(self, slot, n, src, dst, b):
            at = self.base + slot
            return remote(src, dst, col_send.at[at, n], col_recv.at[at, n], {"depth": partner(b)})

        def sent(self):
            for n in range(blocks):
                self.rs[n].wait_send()
                self.ag[n].wait_send()
                for level in self.hops:
                    for hop in level[n]:
                        hop.wait_send()

    prefix = Exchange(0, slab, own, pooled, sums, message, landed, lambda n: slab.at[pl.ds(own, half), span(n)], above)
    maxima = Exchange(
        2 + steps * groups, peak, own, mpool.at[0], mpool.at[1], mpool.at[pl.ds(2, steps)], mland,
        lambda n: mpool.at[1 + steps, :, span(n)], proj,
    )

    for n in range(blocks):
        get_ext[n].wait()

        def slab_sum(at, n=n):
            total = ext[0, at, span(n)]
            for p in range(1, planes):
                total = total + ext[p, at, span(n)]
            slab[at, span(n)] = total

        over(rows, slab_sum)
        if n == 0:
            pl.semaphore_wait(barrier, bits + has_up.astype(jnp.int32) + has_down.astype(jnp.int32))
        prefix.rs[n].start()

    for n in range(blocks):
        prefix.rs[n].wait_recv()

        def pool(at, n=n):
            sums[at, span(n)] = slab[pl.ds(own + at.start, chunk), span(n)] + pooled[at, span(n)]

        over(half, pool)
        for hop in prefix.hops[0][n]:
            hop.start()

    get_est.wait()

    def local_weights(at):
        run = ext[0, at, :]
        local[0, at, :] = est[0, at, :]
        for p in range(1, planes):
            local[p, at, :] = jnp.exp(-run) * est[p, at, :]
            if p < planes - 1:
                run = run + ext[p, at, :]

    over(rows, local_weights, 32)
    lpair = halo_pair(
        local.at[:, pl.ds(0, reach)], local.at[:, pl.ds(rows - reach, reach)], lhalo.at[1], lhalo.at[0],
        lambda i: hal_send.at[i], lambda i: hal_recv.at[i],
    )
    halo_start(lpair)

    strata, length = psf_rows.shape
    highest = lax.Precision.HIGHEST

    def spread_taps(psf, width, place):
        taps = psf[...] / jnp.sum(psf[...], axis=1, keepdims=True)
        tap = lax.broadcasted_iota(jnp.int32, (length, width), 0)
        lane = lax.broadcasted_iota(jnp.int32, (length, width), 1)
        pick = place(tap, lane).astype(jnp.float32)
        return jnp.dot(taps, pick, preferred_element_type=jnp.float32, precision=highest)

    def thirds(tap, lane):
        return (lane == tap) | (lane == tap + wide) | (lane == tap + 2 * wide)

    tall_table[0] = spread_taps(psf_rows, 4 * BLOCK, thirds)
    tall_table[1] = spread_taps(psf_rows, 4 * BLOCK, lambda tap, lane: thirds(length - 1 - tap, lane))

    def around(tap, lane):
        return lane == jnp.where(tap >= reach, tap - reach, tap - reach + 2 * BLOCK)

    flat_table[0] = spread_taps(psf_cols, 2 * BLOCK, lambda tap, lane: around(length - 1 - tap, lane))
    flat_table[1] = spread_taps(psf_cols, 2 * BLOCK, around)

    up_flag = jnp.where(has_up, seams[up], 0).astype(jnp.float32)
    down_flag = jnp.where(has_down, seams[jnp.minimum(t, tile_count - 2)], 0).astype(jnp.float32)
    lane = lax.broadcasted_iota(jnp.int32, (1, 4 * BLOCK), 1)
    third = jnp.where(lane < wide, lane, jnp.where(lane < 2 * wide, lane - wide, lane - 2 * wide))
    scale = jnp.where(third < reach, up_flag, jnp.where(third >= wide - reach, down_flag, 1.0))

    def bands(which):
        def one(p, _):
            i = which * planes + p
            row = stratum[p]
            tall = jnp.broadcast_to(tall_table[which, pl.ds(row, 1), :], (rows, 4 * BLOCK))
            tall = pltpu.roll(tall, 0, 1, stride=1, stride_axis=0) * scale
            high, low = split(tall)
            vband[i] = jnp.where(lane < 2 * wide, high.astype(jnp.float32), low.astype(jnp.float32)).astype(jnp.bfloat16)
            square = jnp.broadcast_to(flat_table[which, pl.ds(row, 1), :], (2 * BLOCK, 2 * BLOCK))
            square = pltpu.roll(square, 0, 1, stride=1, stride_axis=0)[:, :BLOCK]
            high, low = split(square)
            lhigh[i] = high
            llow[i] = low
            return 0

        lax.fori_loop(0, planes, one, 0)

    def absorb_all(s, n):
        for g, order in enumerate(orders):
            prefix.hops[s][n][g].wait_recv()
            upper = bit(order[s]).astype(jnp.float32)
            ascending = s == 0 or order[s] > order[s - 1]

            def absorb(at, g=g, order=order, upper=upper, ascending=ascending):
                at = pl.ds(g * part + at.start, chunk)
                got = landed[s, at, span(n)]
                if s == 0:
                    before = upper * got
                elif ascending:
                    before = carried[at, span(n)] + upper * got
                else:
                    before = carried[at, span(n)] + got
                carried[at, span(n)] = before
                if s + 1 < steps:
                    if order[s + 1] > order[s]:
                        total = (sums[at, span(n)] if s == 0 else message[s - 1, at, span(n)]) + got
                        message[s, at, span(n)] = total
                    else:
                        lower = 1.0 - bit(order[s + 1]).astype(jnp.float32)
                        message[s, at, span(n)] = before + lower * sums[at, span(n)]

            over(part, absorb)
            if s + 1 < steps:
                prefix.hops[s + 1][n][g].start()

    bands(0)
    for m in (mhigh, mlow):
        m[:, :, :SIDE] = jnp.zeros((planes, rows, SIDE), jnp.bfloat16)
        m[:, :, SIDE + cols:] = jnp.zeros((planes, rows, SIDE), jnp.bfloat16)
    for s in range(steps - 1):
        for n in range(blocks):
            absorb_all(s, n)
    bands(1)

    fpairs = [
        halo_pair(
            above.at[pl.ds(0, reach), span(n)], above.at[pl.ds(rows - reach, reach), span(n)],
            fhalo.at[1, :, span(n)], fhalo.at[0, :, span(n)],
            lambda i, n=n: hal_send.at[2 + 2 * n + i], lambda i, n=n: hal_recv.at[2 + 2 * n + i],
        )
        for n in range(blocks)
    ]

    def share(n):
        absorb_all(steps - 1, n)

        def give(at):
            mine = pl.ds(own + at.start, chunk)
            before = carried[at, span(n)]
            above[mine, span(n)] = before + first * pooled[at, span(n)]
            slab[mine, span(n)] = before + (1.0 - first) * slab[mine, span(n)]

        over(half, give)
        prefix.ag[n].start()

    def fade(n):
        prefix.ag[n].wait_recv()

        def one(at):
            above[at, span(n)] = jnp.exp(-above[at, span(n)])

        over(rows, one)
        halo_start(fpairs[n])

    def put(value, start, size):
        high, low = split(value)
        stacked[pl.ds(start, size), :] = high
        stacked[pl.ds(wide + start, size), :] = low
        stacked[pl.ds(2 * wide + start, size), :] = high

    def mix(n, which, edge, inner):
        def one(p, _):
            put(edge(0, p), 0, reach)
            put(edge(1, p), rows + reach, reach)
            over(rows, lambda at: put(inner(p, at), pl.multiple_of(at.start + reach, 32), chunk))
            mixed = jnp.dot(vband[which * planes + p, :, : 3 * wide], stacked[...], preferred_element_type=jnp.float32)
            high, low = split(mixed)
            mhigh[p, :, SIDE + n * BLOCK : SIDE + (n + 1) * BLOCK] = high
            mlow[p, :, SIDE + n * BLOCK : SIDE + (n + 1) * BLOCK] = low
            return 0

        lax.fori_loop(0, planes, one, 0)

    def blurred(n, i, p):
        def window(m):
            start = n * BLOCK
            return jnp.concatenate(
                [m[p, :, start + SIDE : start + SIDE + BLOCK + SIDE], m[p, :, start : start + SIDE]], axis=1
            )

        high, low = window(mhigh), window(mlow)
        return (
            jnp.dot(high, lhigh[i], preferred_element_type=jnp.float32)
            + jnp.dot(low, lhigh[i], preferred_element_type=jnp.float32)
            + jnp.dot(high, llow[i], preferred_element_type=jnp.float32)
        )

    quot = ext

    qpairs = [
        halo_pair(
            quot.at[:, pl.ds(0, reach), span(n)], quot.at[:, pl.ds(rows - reach, reach), span(n)],
            qhalo.at[1, :, :, span(n)], qhalo.at[0, :, :, span(n)],
            lambda i, n=n: q_send.at[i, n], lambda i, n=n: q_recv.at[i, n],
        )
        for n in range(blocks)
    ]

    def forward_mix(n):
        halo_recv(fpairs[n])
        mix(
            n, 0, lambda side, p: fhalo[side, :, span(n)] * lhalo[side, p, :, span(n)],
            lambda p, at: above[at, span(n)] * local[p, at, span(n)],
        )

    def forward_end(n):
        def one(p, _):
            quot[p, :, span(n)] = meas[p, :, span(n)] / blurred(n, p, p)
            return 0

        lax.fori_loop(0, planes, one, 0)
        halo_start(qpairs[n])

    def backward_mix(n):
        halo_recv(qpairs[n])
        mix(n, 1, lambda side, p: qhalo[side, p, :, span(n)], lambda p, at: quot[p, at, span(n)])

    def backward_end(n):
        def one(p, _):
            upd[p, :, span(n)] = est[p, :, span(n)] * blurred(n, planes + p, p)
            return 0

        lax.fori_loop(0, planes, one, 0)

        def top(at):
            best = upd[0, at, span(n)]
            for p in range(1, planes):
                best = jnp.maximum(best, upd[p, at, span(n)])
            peak[at, span(n)] = best

        over(rows, top)
        maxima.rs[n].start()

    share(0)
    for n in range(1, blocks):
        share(n)
        fade(n - 1)
    fade(blocks - 1)
    get_meas.wait()
    halo_recv(lpair)
    forward_mix(0)
    for n in range(1, blocks):
        forward_mix(n)
        forward_end(n - 1)
    forward_end(blocks - 1)

    def raise_up(k, n):
        if k == 0:
            maxima.rs[n].wait_recv()

            def merge(at):
                mpool[1, at, span(n)] = jnp.maximum(mpool[0, at, span(n)], peak[pl.ds(own + at.start, chunk), span(n)])

            over(half, merge)
            for hop in maxima.hops[0][n]:
                hop.start()
            return
        s = k - 1
        for g in range(groups):
            maxima.hops[s][n][g].wait_recv()

            def keep(at, g=g):
                at = pl.ds(g * part + at.start, chunk)
                best = jnp.maximum(mpool[1 + s, at, span(n)], mland[s, at, span(n)])
                if s + 1 < steps:
                    mpool[2 + s, at, span(n)] = best
                else:
                    mpool[1 + steps, at, span(n)] = best
                    proj[pl.ds(own + at.start, chunk), span(n)] = best

            over(part, keep)
            if s + 1 < steps:
                maxima.hops[s + 1][n][g].start()
        if s + 1 == steps:
            maxima.ag[n].start()

    backward_mix(0)
    for n in range(1, blocks + steps + 1):
        if n < blocks:
            backward_mix(n)
        for k in range(steps, -1, -1):
            if 0 <= n - 2 - k < blocks:
                raise_up(k, n - 2 - k)
        if n <= blocks:
            backward_end(n - 1)
    for k in range(steps, -1, -1):
        n = blocks + steps - 1 - k
        if n < blocks:
            raise_up(k, n)
    for n in range(blocks):
        maxima.ag[n].wait_recv()

    prefix.sent()
    maxima.sent()
    halo_sent(lpair)
    for n in range(blocks):
        halo_sent(fpairs[n])
        halo_sent(qpairs[n])


def on_device(dims, measured, estimate, extinction, psf_rows, psf_cols, stratum, seam_flags):
    depth_count, tile_count, planes, rows, cols, reach = dims
    strata, length = psf_rows.shape
    wide = rows + 2 * reach
    blocks = cols // BLOCK
    half = rows // 2
    bits = depth_count.bit_length() - 1
    steps = bits - 1
    groups = 2 if steps == 2 else 1
    collectives = 2 * (2 + steps * groups)
    f32, bf16 = jnp.float32, jnp.bfloat16
    whole = (planes, rows, cols)
    return pl.pallas_call(
        functools.partial(kernel, dims),
        out_shape=(jax.ShapeDtypeStruct(whole, f32), jax.ShapeDtypeStruct((rows, cols), f32)),
        in_specs=[
            pl.BlockSpec(memory_space=pltpu.VMEM),
            pl.BlockSpec(memory_space=pltpu.VMEM),
            pl.BlockSpec(memory_space=pltpu.SMEM),
            pl.BlockSpec(memory_space=pltpu.SMEM),
            pl.BlockSpec(memory_space=pl.ANY),
            pl.BlockSpec(memory_space=pl.ANY),
            pl.BlockSpec(memory_space=pl.ANY),
        ],
        out_specs=(pl.BlockSpec(memory_space=pltpu.VMEM), pl.BlockSpec(memory_space=pltpu.VMEM)),
        scratch_shapes=[
            pltpu.VMEM(whole, f32),
            pltpu.VMEM(whole, f32),
            pltpu.VMEM(whole, f32),
            pltpu.VMEM(whole, f32),
            pltpu.VMEM((3 * wide, BLOCK), bf16),
            pltpu.VMEM((2, strata, 4 * BLOCK), f32),
            pltpu.VMEM((2, strata, 2 * BLOCK), f32),
            pltpu.VMEM((2 * planes, rows, 4 * BLOCK), bf16),
            pltpu.VMEM((2 * planes, 2 * BLOCK, BLOCK), bf16),
            pltpu.VMEM((2 * planes, 2 * BLOCK, BLOCK), bf16),
            pltpu.VMEM((planes, rows, cols + 2 * SIDE), bf16),
            pltpu.VMEM((planes, rows, cols + 2 * SIDE), bf16),
            pltpu.VMEM((rows, cols), f32),
            pltpu.VMEM((half, cols), f32),
            pltpu.VMEM((half, cols), f32),
            pltpu.VMEM((half, cols), f32),
            pltpu.VMEM((max(steps - 1, 1), half, cols), f32),
            pltpu.VMEM((steps, half, cols), f32),
            pltpu.VMEM((rows, cols), f32),
            pltpu.VMEM((rows, cols), f32),
            pltpu.VMEM((2 + steps, half, cols), f32),
            pltpu.VMEM((steps, half, cols), f32),
            pltpu.VMEM((2, planes, reach, cols), f32),
            pltpu.VMEM((2, reach, cols), f32),
            pltpu.VMEM((2, planes, reach, cols), f32),
            pltpu.SemaphoreType.DMA((2 + blocks,)),
            pltpu.SemaphoreType.DMA((2 + 2 * blocks,)),
            pltpu.SemaphoreType.DMA((2 + 2 * blocks,)),
            pltpu.SemaphoreType.DMA((2, blocks)),
            pltpu.SemaphoreType.DMA((2, blocks)),
            pltpu.SemaphoreType.DMA((collectives, blocks)),
            pltpu.SemaphoreType.DMA((collectives, blocks)),
        ],
        compiler_params=pltpu.CompilerParams(
            collective_id=0, has_side_effects=True, vmem_limit_bytes=46 * 1024 * 1024
        ),
    )(psf_rows, psf_cols, stratum, seam_flags, measured, estimate, extinction)


def solution(mesh):
    def body(measured, estimate, extinction, psf_rows, psf_cols, stratum, seam_flags):
        planes, rows, cols = measured.shape
        dims = (mesh.shape["depth"], mesh.shape["tile"], planes, rows, cols, (psf_rows.shape[1] - 1) // 2)
        return on_device(dims, measured, estimate, extinction, psf_rows, psf_cols, stratum, seam_flags)

    return jax.shard_map(
        body,
        mesh=mesh,
        in_specs=(
            P("depth", "tile", None),
            P("depth", "tile", None),
            P("depth", "tile", None),
            P(),
            P(),
            P("depth"),
            P(),
        ),
        out_specs=(P("depth", "tile", None), P("tile", None)),
        check_vma=False,
    )
```

```python
import functools

import jax
import jax.numpy as jnp
from jax import lax
from jax.experimental import pallas as pl
from jax.experimental.pallas import tpu as pltpu
from jax.sharding import PartitionSpec as P

MESH = pl.DeviceIdType.MESH
BLOCK = 256
SIDE = 128


def split(value):
    high = value.astype(jnp.bfloat16)
    low = (value - high.astype(jnp.float32)).astype(jnp.bfloat16)
    return high, low


def kernel(
    dims, psf_rows_hbm, psf_cols_hbm, stratum, seams, meas_hbm, est_hbm, ext_hbm, upd, proj,
    psf_rows, psf_cols, meas, est, ext, local, stacked, tall_table, flat_table, vband, lhigh, llow, mhigh, mlow,
    slab, pooled, carried, sums, message, landed, above, peak, mpool, mland,
    lhalo, fhalo, qhalo,
    in_sem, hal_send, hal_recv, q_send, q_recv, col_send, col_recv,
):
    depth_count, tile_count, planes, rows, cols, reach = dims
    half = rows // 2
    bits = depth_count.bit_length() - 1
    rest = list(range(1, bits))
    orders = [rest, rest[::-1]] if len(rest) == 2 else [rest]
    part = half // len(orders)
    steps = len(rest)
    wide = rows + 2 * reach
    chunk = 64
    blocks = cols // BLOCK
    groups = len(orders)
    d = lax.axis_index("depth")
    t = lax.axis_index("tile")
    has_up = t > 0
    has_down = t < tile_count - 1
    up = jnp.maximum(t - 1, 0)
    down = jnp.minimum(t + 1, tile_count - 1)

    def bit(b):
        return (d // (1 << b)) % 2

    def partner(b):
        return d + (1 - 2 * bit(b)) * (1 << b)

    def loads(which, src, dst):
        return pltpu.make_async_copy(src, dst, in_sem.at[which])

    def span(n):
        return pl.ds(n * BLOCK, BLOCK)

    get_ext = [loads(2 + n, ext_hbm.at[:, :, span(n)], ext.at[:, :, span(n)]) for n in range(blocks)]
    get_est = loads(0, est_hbm, est)
    get_meas = loads(1, meas_hbm, meas)
    get_rows = loads(2 + blocks, psf_rows_hbm, psf_rows)
    get_cols = loads(3 + blocks, psf_cols_hbm, psf_cols)
    for n in range(blocks):
        get_ext[n].start()
    get_rows.start()
    get_cols.start()
    get_est.start()
    get_meas.start()

    barrier = pltpu.get_barrier_semaphore()
    for b in range(bits):
        pl.semaphore_signal(barrier, inc=1, device_id={"depth": partner(b)}, device_id_type=MESH)

    @pl.when(has_up)
    def _():
        pl.semaphore_signal(barrier, inc=1, device_id={"tile": up}, device_id_type=MESH)

    @pl.when(has_down)
    def _():
        pl.semaphore_signal(barrier, inc=1, device_id={"tile": down}, device_id_type=MESH)

    def remote(src, dst, send, recv, where):
        return pltpu.make_async_remote_copy(
            src_ref=src, dst_ref=dst, send_sem=send, recv_sem=recv, device_id=where, device_id_type=MESH
        )

    def halo_pair(head, tail, to_up, to_down, send, recv):
        return (
            remote(head, to_up, send(0), recv(1), {"tile": up}),
            remote(tail, to_down, send(1), recv(0), {"tile": down}),
        )

    def halo_start(pair):
        pl.when(has_up)(lambda: pair[0].start())
        pl.when(has_down)(lambda: pair[1].start())

    def halo_recv(pair):
        pl.when(has_up)(lambda: pair[1].wait_recv())
        pl.when(has_down)(lambda: pair[0].wait_recv())

    def halo_sent(pair):
        pl.when(has_up)(lambda: pair[0].wait_send())
        pl.when(has_down)(lambda: pair[1].wait_send())

    @pl.when(t == 0)
    def _():
        lhalo[0] = jnp.zeros(lhalo.shape[1:], jnp.float32)
        fhalo[0] = jnp.zeros(fhalo.shape[1:], jnp.float32)
        qhalo[0] = jnp.zeros(qhalo.shape[1:], jnp.float32)

    @pl.when(t == tile_count - 1)
    def _():
        lhalo[1] = jnp.zeros(lhalo.shape[1:], jnp.float32)
        fhalo[1] = jnp.zeros(fhalo.shape[1:], jnp.float32)
        qhalo[1] = jnp.zeros(qhalo.shape[1:], jnp.float32)

    def over(count, body, size=chunk):
        def one(i, _):
            body(pl.ds(pl.multiple_of(i * size, size), size))
            return 0

        if count // size <= 4:
            for i in range(count // size):
                body(pl.ds(i * size, size))
        else:
            lax.fori_loop(0, count // size, one, 0)

    core = bit(0)
    own = pl.multiple_of(core * half, half)
    other = pl.multiple_of((1 - core) * half, half)
    first = core.astype(jnp.float32)

    class Exchange:
        def __init__(self, base, source, mine, pooled, lead, relay, landed, finish, target):
            self.base = base
            self.rs = [self.copy(0, n, source.at[pl.ds(other, half), span(n)], pooled.at[:, span(n)], 0) for n in range(blocks)]
            self.hops = []
            for s in range(steps):
                level = []
                for n in range(blocks):
                    row = []
                    for g, order in enumerate(orders):
                        where = pl.ds(g * part, part)
                        src = relay.at[s - 1, where, span(n)] if s else lead.at[where, span(n)]
                        row.append(self.copy(2 + s * groups + g, n, src, landed.at[s, where, span(n)], order[s]))
                    level.append(row)
                self.hops.append(level)
            self.ag = [self.copy(1, n, finish(n), target.at[pl.ds(own, half), span(n)], 0) for n in range(blocks)]

        def copy(self, slot, n, src, dst, b):
            at = self.base + slot
            return remote(src, dst, col_send.at[at, n], col_recv.at[at, n], {"depth": partner(b)})

        def sent(self):
            for n in range(blocks):
                self.rs[n].wait_send()
                self.ag[n].wait_send()
                for level in self.hops:
                    for hop in level[n]:
                        hop.wait_send()

    prefix = Exchange(0, slab, own, pooled, sums, message, landed, lambda n: slab.at[pl.ds(own, half), span(n)], above)
    maxima = Exchange(
        2 + steps * groups, peak, own, mpool.at[0], mpool.at[1], mpool.at[pl.ds(2, steps)], mland,
        lambda n: mpool.at[1 + steps, :, span(n)], proj,
    )

    for n in range(blocks):
        get_ext[n].wait()

        def slab_sum(at, n=n):
            total = ext[0, at, span(n)]
            for p in range(1, planes):
                total = total + ext[p, at, span(n)]
            slab[at, span(n)] = total

        over(rows, slab_sum)
        if n == 0:
            pl.semaphore_wait(barrier, bits + has_up.astype(jnp.int32) + has_down.astype(jnp.int32))
        prefix.rs[n].start()

    for n in range(blocks):
        prefix.rs[n].wait_recv()

        def pool(at, n=n):
            sums[at, span(n)] = slab[pl.ds(own + at.start, chunk), span(n)] + pooled[at, span(n)]

        over(half, pool)
        for hop in prefix.hops[0][n]:
            hop.start()

    get_est.wait()

    def local_weights(at):
        run = ext[0, at, :]
        local[0, at, :] = est[0, at, :]
        for p in range(1, planes):
            local[p, at, :] = jnp.exp(-run) * est[p, at, :]
            if p < planes - 1:
                run = run + ext[p, at, :]

    over(rows, local_weights, 32)
    lpair = halo_pair(
        local.at[:, pl.ds(0, reach)], local.at[:, pl.ds(rows - reach, reach)], lhalo.at[1], lhalo.at[0],
        lambda i: hal_send.at[i], lambda i: hal_recv.at[i],
    )
    halo_start(lpair)

    get_rows.wait()
    get_cols.wait()
    strata, length = psf_rows.shape
    highest = lax.Precision.HIGHEST

    def spread_taps(psf, width, place):
        taps = psf[...] / jnp.sum(psf[...], axis=1, keepdims=True)
        tap = lax.broadcasted_iota(jnp.int32, (length, width), 0)
        lane = lax.broadcasted_iota(jnp.int32, (length, width), 1)
        pick = place(tap, lane).astype(jnp.float32)
        return jnp.dot(taps, pick, preferred_element_type=jnp.float32, precision=highest)

    def thirds(tap, lane):
        return (lane == tap) | (lane == tap + wide) | (lane == tap + 2 * wide)

    tall_table[0] = spread_taps(psf_rows, 4 * BLOCK, thirds)
    tall_table[1] = spread_taps(psf_rows, 4 * BLOCK, lambda tap, lane: thirds(length - 1 - tap, lane))

    def around(tap, lane):
        return lane == jnp.where(tap >= reach, tap - reach, tap - reach + 2 * BLOCK)

    flat_table[0] = spread_taps(psf_cols, 2 * BLOCK, lambda tap, lane: around(length - 1 - tap, lane))
    flat_table[1] = spread_taps(psf_cols, 2 * BLOCK, around)

    up_flag = jnp.where(has_up, seams[up], 0).astype(jnp.float32)
    down_flag = jnp.where(has_down, seams[jnp.minimum(t, tile_count - 2)], 0).astype(jnp.float32)
    lane = lax.broadcasted_iota(jnp.int32, (1, 4 * BLOCK), 1)
    third = jnp.where(lane < wide, lane, jnp.where(lane < 2 * wide, lane - wide, lane - 2 * wide))
    scale = jnp.where(third < reach, up_flag, jnp.where(third >= wide - reach, down_flag, 1.0))

    def bands(which):
        def one(p, _):
            i = which * planes + p
            row = stratum[p]
            tall = jnp.broadcast_to(tall_table[which, pl.ds(row, 1), :], (rows, 4 * BLOCK))
            tall = pltpu.roll(tall, 0, 1, stride=1, stride_axis=0) * scale
            high, low = split(tall)
            vband[i] = jnp.where(lane < 2 * wide, high.astype(jnp.float32), low.astype(jnp.float32)).astype(jnp.bfloat16)
            square = jnp.broadcast_to(flat_table[which, pl.ds(row, 1), :], (2 * BLOCK, 2 * BLOCK))
            square = pltpu.roll(square, 0, 1, stride=1, stride_axis=0)[:, :BLOCK]
            high, low = split(square)
            lhigh[i] = high
            llow[i] = low
            return 0

        lax.fori_loop(0, planes, one, 0)

    def absorb_all(s, n):
        for g, order in enumerate(orders):
            prefix.hops[s][n][g].wait_recv()
            upper = bit(order[s]).astype(jnp.float32)
            ascending = s == 0 or order[s] > order[s - 1]

            def absorb(at, g=g, order=order, upper=upper, ascending=ascending):
                at = pl.ds(g * part + at.start, chunk)
                got = landed[s, at, span(n)]
                if s == 0:
                    before = upper * got
                elif ascending:
                    before = carried[at, span(n)] + upper * got
                else:
                    before = carried[at, span(n)] + got
                carried[at, span(n)] = before
                if s + 1 < steps:
                    if order[s + 1] > order[s]:
                        total = (sums[at, span(n)] if s == 0 else message[s - 1, at, span(n)]) + got
                        message[s, at, span(n)] = total
                    else:
                        lower = 1.0 - bit(order[s + 1]).astype(jnp.float32)
                        message[s, at, span(n)] = before + lower * sums[at, span(n)]

            over(part, absorb)
            if s + 1 < steps:
                prefix.hops[s + 1][n][g].start()

    bands(0)
    for m in (mhigh, mlow):
        m[:, :, :SIDE] = jnp.zeros((planes, rows, SIDE), jnp.bfloat16)
        m[:, :, SIDE + cols:] = jnp.zeros((planes, rows, SIDE), jnp.bfloat16)
    for s in range(steps - 1):
        for n in range(blocks):
            absorb_all(s, n)
    bands(1)

    fpairs = [
        halo_pair(
            above.at[pl.ds(0, reach), span(n)], above.at[pl.ds(rows - reach, reach), span(n)],
            fhalo.at[1, :, span(n)], fhalo.at[0, :, span(n)],
            lambda i, n=n: hal_send.at[2 + 2 * n + i], lambda i, n=n: hal_recv.at[2 + 2 * n + i],
        )
        for n in range(blocks)
    ]

    def share(n):
        absorb_all(steps - 1, n)

        def give(at):
            mine = pl.ds(own + at.start, chunk)
            before = carried[at, span(n)]
            above[mine, span(n)] = before + first * pooled[at, span(n)]
            slab[mine, span(n)] = before + (1.0 - first) * slab[mine, span(n)]

        over(half, give)
        prefix.ag[n].start()

    def fade(n):
        prefix.ag[n].wait_recv()

        def one(at):
            above[at, span(n)] = jnp.exp(-above[at, span(n)])

        over(rows, one)
        halo_start(fpairs[n])

    def put(value, start, size):
        high, low = split(value)
        stacked[pl.ds(start, size), :] = high
        stacked[pl.ds(wide + start, size), :] = low
        stacked[pl.ds(2 * wide + start, size), :] = high

    def mix(n, which, edge, inner):
        def one(p, _):
            put(edge(0, p), 0, reach)
            put(edge(1, p), rows + reach, reach)
            over(rows, lambda at: put(inner(p, at), at.start + reach, chunk))
            mixed = jnp.dot(vband[which * planes + p, :, : 3 * wide], stacked[...], preferred_element_type=jnp.float32)
            high, low = split(mixed)
            mhigh[p, :, SIDE + n * BLOCK : SIDE + (n + 1) * BLOCK] = high
            mlow[p, :, SIDE + n * BLOCK : SIDE + (n + 1) * BLOCK] = low
            return 0

        lax.fori_loop(0, planes, one, 0)

    def blurred(n, i, p):
        def window(m):
            start = n * BLOCK
            return jnp.concatenate(
                [m[p, :, start + SIDE : start + SIDE + BLOCK + SIDE], m[p, :, start : start + SIDE]], axis=1
            )

        high, low = window(mhigh), window(mlow)
        return (
            jnp.dot(high, lhigh[i], preferred_element_type=jnp.float32)
            + jnp.dot(low, lhigh[i], preferred_element_type=jnp.float32)
            + jnp.dot(high, llow[i], preferred_element_type=jnp.float32)
        )

    quot = ext

    qpairs = [
        halo_pair(
            quot.at[:, pl.ds(0, reach), span(n)], quot.at[:, pl.ds(rows - reach, reach), span(n)],
            qhalo.at[1, :, :, span(n)], qhalo.at[0, :, :, span(n)],
            lambda i, n=n: q_send.at[i, n], lambda i, n=n: q_recv.at[i, n],
        )
        for n in range(blocks)
    ]

    def forward_mix(n):
        halo_recv(fpairs[n])
        mix(
            n, 0, lambda side, p: fhalo[side, :, span(n)] * lhalo[side, p, :, span(n)],
            lambda p, at: above[at, span(n)] * local[p, at, span(n)],
        )

    def forward_end(n):
        def one(p, _):
            quot[p, :, span(n)] = meas[p, :, span(n)] / blurred(n, p, p)
            return 0

        lax.fori_loop(0, planes, one, 0)
        halo_start(qpairs[n])

    def backward_mix(n):
        halo_recv(qpairs[n])
        mix(n, 1, lambda side, p: qhalo[side, p, :, span(n)], lambda p, at: quot[p, at, span(n)])

    def backward_end(n):
        def one(p, _):
            upd[p, :, span(n)] = est[p, :, span(n)] * blurred(n, planes + p, p)
            return 0

        lax.fori_loop(0, planes, one, 0)

        def top(at):
            best = upd[0, at, span(n)]
            for p in range(1, planes):
                best = jnp.maximum(best, upd[p, at, span(n)])
            peak[at, span(n)] = best

        over(rows, top)
        maxima.rs[n].start()

    share(0)
    for n in range(1, blocks):
        share(n)
        fade(n - 1)
    fade(blocks - 1)
    get_meas.wait()
    halo_recv(lpair)
    forward_mix(0)
    for n in range(1, blocks):
        forward_mix(n)
        forward_end(n - 1)
    forward_end(blocks - 1)

    def raise_up(k, n):
        if k == 0:
            maxima.rs[n].wait_recv()

            def merge(at):
                mpool[1, at, span(n)] = jnp.maximum(mpool[0, at, span(n)], peak[pl.ds(own + at.start, chunk), span(n)])

            over(half, merge)
            for hop in maxima.hops[0][n]:
                hop.start()
            return
        s = k - 1
        for g in range(groups):
            maxima.hops[s][n][g].wait_recv()

            def keep(at, g=g):
                at = pl.ds(g * part + at.start, chunk)
                best = jnp.maximum(mpool[1 + s, at, span(n)], mland[s, at, span(n)])
                if s + 1 < steps:
                    mpool[2 + s, at, span(n)] = best
                else:
                    mpool[1 + steps, at, span(n)] = best
                    proj[pl.ds(own + at.start, chunk), span(n)] = best

            over(part, keep)
            if s + 1 < steps:
                maxima.hops[s + 1][n][g].start()
        if s + 1 == steps:
            maxima.ag[n].start()

    backward_mix(0)
    for n in range(1, blocks + steps + 1):
        if n < blocks:
            backward_mix(n)
        for k in range(steps, -1, -1):
            if 0 <= n - 2 - k < blocks:
                raise_up(k, n - 2 - k)
        if n <= blocks:
            backward_end(n - 1)
    for k in range(steps, -1, -1):
        n = blocks + steps - 1 - k
        if n < blocks:
            raise_up(k, n)
    for n in range(blocks):
        maxima.ag[n].wait_recv()

    prefix.sent()
    maxima.sent()
    halo_sent(lpair)
    for n in range(blocks):
        halo_sent(fpairs[n])
        halo_sent(qpairs[n])


def on_device(dims, measured, estimate, extinction, psf_rows, psf_cols, stratum, seam_flags):
    depth_count, tile_count, planes, rows, cols, reach = dims
    strata, length = psf_rows.shape
    wide = rows + 2 * reach
    blocks = cols // BLOCK
    half = rows // 2
    bits = depth_count.bit_length() - 1
    steps = bits - 1
    groups = 2 if steps == 2 else 1
    collectives = 2 * (2 + steps * groups)
    f32, bf16 = jnp.float32, jnp.bfloat16
    whole = (planes, rows, cols)
    return pl.pallas_call(
        functools.partial(kernel, dims),
        out_shape=(jax.ShapeDtypeStruct(whole, f32), jax.ShapeDtypeStruct((rows, cols), f32)),
        in_specs=[
            pl.BlockSpec(memory_space=pltpu.HBM),
            pl.BlockSpec(memory_space=pltpu.HBM),
            pl.BlockSpec(memory_space=pltpu.SMEM),
            pl.BlockSpec(memory_space=pltpu.SMEM),
            pl.BlockSpec(memory_space=pl.ANY),
            pl.BlockSpec(memory_space=pl.ANY),
            pl.BlockSpec(memory_space=pl.ANY),
        ],
        out_specs=(pl.BlockSpec(memory_space=pltpu.VMEM), pl.BlockSpec(memory_space=pltpu.VMEM)),
        scratch_shapes=[
            pltpu.VMEM((strata, length), f32),
            pltpu.VMEM((strata, length), f32),
            pltpu.VMEM(whole, f32),
            pltpu.VMEM(whole, f32),
            pltpu.VMEM(whole, f32),
            pltpu.VMEM(whole, f32),
            pltpu.VMEM((3 * wide, BLOCK), bf16),
            pltpu.VMEM((2, strata, 4 * BLOCK), f32),
            pltpu.VMEM((2, strata, 2 * BLOCK), f32),
            pltpu.VMEM((2 * planes, rows, 4 * BLOCK), bf16),
            pltpu.VMEM((2 * planes, 2 * BLOCK, BLOCK), bf16),
            pltpu.VMEM((2 * planes, 2 * BLOCK, BLOCK), bf16),
            pltpu.VMEM((planes, rows, cols + 2 * SIDE), bf16),
            pltpu.VMEM((planes, rows, cols + 2 * SIDE), bf16),
            pltpu.VMEM((rows, cols), f32),
            pltpu.VMEM((half, cols), f32),
            pltpu.VMEM((half, cols), f32),
            pltpu.VMEM((half, cols), f32),
            pltpu.VMEM((max(steps - 1, 1), half, cols), f32),
            pltpu.VMEM((steps, half, cols), f32),
            pltpu.VMEM((rows, cols), f32),
            pltpu.VMEM((rows, cols), f32),
            pltpu.VMEM((2 + steps, half, cols), f32),
            pltpu.VMEM((steps, half, cols), f32),
            pltpu.VMEM((2, planes, reach, cols), f32),
            pltpu.VMEM((2, reach, cols), f32),
            pltpu.VMEM((2, planes, reach, cols), f32),
            pltpu.SemaphoreType.DMA((4 + blocks,)),
            pltpu.SemaphoreType.DMA((2 + 2 * blocks,)),
            pltpu.SemaphoreType.DMA((2 + 2 * blocks,)),
            pltpu.SemaphoreType.DMA((2, blocks)),
            pltpu.SemaphoreType.DMA((2, blocks)),
            pltpu.SemaphoreType.DMA((collectives, blocks)),
            pltpu.SemaphoreType.DMA((collectives, blocks)),
        ],
        compiler_params=pltpu.CompilerParams(
            collective_id=0, has_side_effects=True, vmem_limit_bytes=46 * 1024 * 1024
        ),
    )(psf_rows, psf_cols, stratum, seam_flags, measured, estimate, extinction)


def solution(mesh):
    def body(measured, estimate, extinction, psf_rows, psf_cols, stratum, seam_flags):
        planes, rows, cols = measured.shape
        dims = (mesh.shape["depth"], mesh.shape["tile"], planes, rows, cols, (psf_rows.shape[1] - 1) // 2)
        return on_device(dims, measured, estimate, extinction, psf_rows, psf_cols, stratum, seam_flags)

    return jax.shard_map(
        body,
        mesh=mesh,
        in_specs=(
            P("depth", "tile", None),
            P("depth", "tile", None),
            P("depth", "tile", None),
            P(),
            P(),
            P("depth"),
            P(),
        ),
        out_specs=(P("depth", "tile", None), P("tile", None)),
        check_vma=False,
    )
```
